32 devices in a mesh: psg: 8 (over z, x), mp: 4 (over y, core).
Axes of the slice: x: 2, y: 2, z: 4, core: 2. Of those that a mesh axis runs over, the one named last changes fastest.
Arguments:
- tokens: bfloat16 [8192, 4096], P('psg'), may hold values from -6 to 6
- lengths: int32 [32], P('psg'), may hold values from 32 to 256, as said below
- assignment: int32 [32], P('psg'), may hold values from 0 to 3, as said below
- retrieval: float32 [32], P('psg'), may hold values from -8 to 306
- enc_gain: float32 [4096], replicated, may hold values from 0.25 to 1.75
- enc_qkv: bfloat16 [3, 4096, 2048], P(None, 'psg', 'mp'), may hold values from -0.09375 to 0.09375
- position_bias: float32 [32, 32], P('mp'), may hold values from -6 to 306
- enc_output: bfloat16 [2048, 4096], P('mp', 'psg'), may hold values from -0.125 to 0.125
- final_gain: float32 [4096], replicated, may hold values from 0.25 to 1.75
- embedding: bfloat16 [32128, 4096], P('mp', 'psg'), may hold values from -18 to 18
- dec_tokens: int32 [4, 2], replicated, may hold values from 0 to 32127
- dec_gain: float32 [4096], P('psg'), may hold values from 0.25 to 1.75
- cross_query: bfloat16 [4096, 2048], P('psg', 'mp'), may hold values from -0.0234375 to 0.0234375
- cross_keyval: bfloat16 [2, 4096, 2048], P(None, 'psg', 'mp'), may hold values from -0.09375 to 0.09375
- cross_output: bfloat16 [2048, 4096], P('mp', 'psg'), may hold values from -0.25 to 0.25
Outputs:
- encoded: bfloat16 [8192, 4096], P('psg', 'mp')
- decoded: bfloat16 [4, 2, 4096], P(None, None, ('psg', 'mp'))
The draws below stay inside these ranges and needn't reach their ends.
Inputs may be any that keep to these rules, and one draw needn't show every extreme that they name: Passage p holds real tokens in its first lengths[p] slots and padding after them; in every draw all passages of some index of psg have 256 real tokens. `assignment`: every claim has exactly 8 passages.
All inputs are finite; a program needn't handle non-finite values.
Results may differ from the reference program's by a relative error of at most 0.013.
The reference program's roundings to bfloat16 on the way count: a program that leaves them out, or rounds other values in their place, can miss the bound.
Values may be sent and summed in bfloat16 or wider, within the bound.
No kernel may reach another device: no remote copies, remote signals or barrier semaphores. Data moves between devices by JAX's collectives and lax.ppermute only.
A program may use at most 128 MiB of HBM per device.

```python
import math
import jax
import jax.numpy as jnp
import numpy as np
from jax import lax

D = 4096
HEAD_DIM = 64
VOCAB = 32128
BUCKETS = 32
MAXDIST = 128
HEADS = 32
SEQ = 256
CLAIMS = 4
POS = 2
PSG_DEV = 4
PASSAGES = 32
TOKENS = 8192
PSG_CLAIM = 8
INNER = 2048
N_MP = 4


def claim_table(key):
    order = jax.random.permutation(jax.random.fold_in(key, 11), PASSAGES)
    return (order // PSG_CLAIM).astype(jnp.int32)


def draw_assignment(key, part):
    return claim_table(key)


def draw_retrieval(key, part):
    noise = jax.random.normal(jax.random.fold_in(key, 12), (PASSAGES,), jnp.float32)
    return jnp.clip(2.0 * noise, -8.0, 8.0)


def draw_lengths(key, part):
    lengths = jax.random.randint(jax.random.fold_in(key, 21), (PASSAGES,), SEQ // 8, SEQ + 1)
    devices = PASSAGES // PSG_DEV
    full_device = jax.random.randint(jax.random.fold_in(key, 22), (), 0, devices)
    position = jnp.arange(PASSAGES)
    lengths = jnp.where(position // PSG_DEV == full_device, SEQ, lengths)
    shortest = (full_device + 1) % devices * PSG_DEV
    lengths = jnp.where(position == shortest, SEQ // 8, lengths)
    return lengths.astype(jnp.int32)


def draw_position_bias(key, part):
    noise = jax.random.normal(jax.random.fold_in(key, 31), (HEADS, BUCKETS), jnp.float32)
    return jnp.clip(noise, -4.0, 4.0)


def draw_embedding(key, part):
    column = jnp.arange(D, dtype=jnp.float32)[None, :] / D
    col_scale = jnp.exp(column * jnp.log(3.0)) * jnp.exp(jax.random.uniform(jax.random.fold_in(key, 41), (1, D), jnp.float32, 0.0, jnp.log(3.0)))
    row_scale = jnp.exp(jax.random.uniform(jax.random.fold_in(key, 42), (VOCAB, 1), jnp.float32, 0.0, jnp.log(4.0)))
    base = jnp.clip(jax.random.normal(jax.random.fold_in(key, 45), (VOCAB, D), jnp.float32), -4.0, 4.0)
    return (0.12 * base * row_scale * col_scale).astype(jnp.bfloat16)


def plant(drawn, rng, least, high):
    extent = drawn.shape
    place = [jax.random.randint(jax.random.fold_in(rng, axis), (), 0, extent[axis]) for axis in range(len(extent))]
    drawn = drawn.at[tuple(place)].set(least)
    longest = extent.index(max(extent))
    place[longest] = (place[longest] + 1) % extent[longest]
    return drawn.at[tuple(place)].set(high)


def shard_levels(key, shape, shards, least, high):
    factor_of = 1.0
    for axis_at, shards_of in shards:
        draws = jax.random.uniform(jax.random.fold_in(jax.random.fold_in(key, 6), axis_at), (shards_of,), jnp.float32, least / len(shards), high / len(shards))
        factor_of = factor_of * jnp.repeat(jnp.exp(draws), shape[axis_at] // shards_of).reshape((-1,) + (1,) * (len(shape) - 1 - axis_at))
    return factor_of


def cumulative_ranks(count, lean):
    loads = [(1 << 20) // math.isqrt(standing ** lean) + 1 for standing in range(1, count + 1)]
    deviation = 1 + sum(loads) // (1 << 30)
    return np.cumsum(np.array([max(1, weight // deviation) for weight in loads]))


def ranked_ids(stream_key, dims, count, skew):
    grid = cumulative_ranks(count, skew)
    lot = jax.random.randint(jax.random.fold_in(stream_key, 1), dims, 0, int(grid[count - 1]))
    rank = jnp.searchsorted(jnp.asarray(grid, jnp.int32), lot, side="right")
    return jax.random.permutation(jax.random.fold_in(stream_key, 2), count)[rank].astype(jnp.int32)


def scatter_about(rng, shape, scale, reach, shards=(), kind=jnp.bfloat16):
    values = jax.random.normal(rng, shape, jnp.float32) * scale
    if len(shards) > 0:
        values = shard_levels(rng, shape, shards, -0.22, 0.18) * values
    return jnp.clip(values, min=-reach, max=reach).astype(kind)


def setup_inputs(seed: int = 0) -> dict:
    seeds = jax.random.split(jax.random.key(seed), 16)
    tokens = scatter_about(seeds[0], (TOKENS, D), 1.0, 6.0, ((0, 8),))
    lengths = draw_lengths(jax.random.fold_in(seeds[15], 71), 0)
    assignment = draw_assignment(jax.random.fold_in(seeds[15], 71), 0)
    retrieval = draw_retrieval(jax.random.fold_in(seeds[15], 71), 0)
    enc_gain = jnp.clip(1.0 + 0.15 * jax.random.normal(seeds[4], (D,), jnp.float32), 0.25, 1.75)
    enc_qkv = scatter_about(seeds[5], (3, D, INNER), D ** -0.5, 0.09375, ((1, 8), (2, 4)))
    position_bias = draw_position_bias(jax.random.fold_in(seeds[15], 71), 0)
    enc_output = scatter_about(seeds[7], (INNER, D), INNER ** -0.5, 0.125, ((0, 4), (1, 8)))
    final_gain = jnp.clip(1.0 + 0.15 * jax.random.normal(seeds[8], (D,), jnp.float32), 0.25, 1.75)
    embedding = draw_embedding(jax.random.fold_in(seeds[15], 71), 0)
    dec_tokens = plant(ranked_ids(seeds[10], (CLAIMS, POS), VOCAB, 2), jax.random.fold_in(seeds[10], 3), 0, VOCAB - 1).astype(jnp.int32)
    dec_gain = jnp.clip(1.0 + 0.15 * jax.random.normal(seeds[11], (D,), jnp.float32), 0.25, 1.75)
    cross_query = scatter_about(seeds[12], (D, INNER), (16 * D) ** -0.5, 0.0234375, ((0, 8), (1, 4)))
    cross_keyval = scatter_about(seeds[13], (2, D, INNER), D ** -0.5, 0.09375, ((1, 8), (2, 4)))
    cross_output = scatter_about(seeds[14], (INNER, D), (INNER // 4) ** -0.5, 0.25, ((0, 4), (1, 8)))
    return {"tokens": tokens, "lengths": lengths, "assignment": assignment, "retrieval": retrieval, "enc_gain": enc_gain, "enc_qkv": enc_qkv, "position_bias": position_bias, "enc_output": enc_output, "final_gain": final_gain, "embedding": embedding, "dec_tokens": dec_tokens, "dec_gain": dec_gain, "cross_query": cross_query, "cross_keyval": cross_keyval, "cross_output": cross_output}


EPSILON = 1e-06
MASKED = -1e+30
HIGHEST = lax.Precision.HIGHEST

def bucket_onehot(length, buckets, max_distance):
    halfway = buckets // 2
    exact_max = halfway // 2
    relative_list = list(range(-(length - 1), length))
    beyond_list = [min(halfway - 1, exact_max + math.floor(math.log(max(abs(shift), 1) / exact_max) / math.log(max_distance / exact_max) * (halfway - exact_max))) for shift in relative_list]
    relative = np.array(relative_list)
    beyond = np.array(beyond_list)
    distance = np.abs(relative)
    bucket_ids = np.where(relative > 0, halfway, 0) + np.where(distance < exact_max, distance, beyond)
    return (bucket_ids[None, :] == np.arange(buckets)[:, None]).astype(np.float32)

def toeplitz(vectors):
    heads_count, width_all = vectors.shape
    length = (width_all + 1) // 2
    padded = jnp.concatenate([vectors, jnp.zeros((heads_count, 1), vectors.dtype)], axis=1)
    rolled = jnp.roll(padded, -(length - 1), axis=1)
    repeated = jnp.tile(rolled, (1, length))[:, :length * (2 * length - 1)]
    return repeated.reshape(heads_count, length, 2 * length - 1)[:, :, :length]

def rms_norm(values, norm_gain):
    values = values.astype(jnp.float32)
    inverse = lax.rsqrt(lax.optimization_barrier(jnp.mean(values * values, axis=-1, keepdims=True)) + EPSILON)
    return values * inverse * norm_gain

def rounded(values):
    return lax.optimization_barrier(values.astype(jnp.bfloat16))

def reference(tokens, lengths, assignment, retrieval, enc_gain, enc_qkv, position_bias, enc_output, final_gain, embedding, dec_tokens, dec_gain, cross_query, cross_keyval, cross_output):
    query_rows = CLAIMS * POS
    group_cols = INNER // N_MP
    bias_table = jnp.dot(position_bias, jnp.asarray(bucket_onehot(SEQ, BUCKETS, MAXDIST)), precision=HIGHEST)
    pair_bias = toeplitz(bias_table)
    out_groups = enc_output.astype(jnp.float32).reshape(N_MP, group_cols, D)
    embedded = embedding[dec_tokens.reshape(-1)]
    dquery = rms_norm(embedded, dec_gain)
    cquery = jnp.dot(dquery, cross_query.astype(jnp.float32), precision=HIGHEST).reshape(query_rows, HEADS, HEAD_DIM)
    row_claim = jnp.arange(query_rows) // POS
    positions = jnp.arange(SEQ)

    def passage_step(state_in, inputs):
        run_max, run_total, run_acc = state_in
        passage, length, owner_claim, score_bias = inputs
        normed = rms_norm(passage, enc_gain).astype(jnp.bfloat16)
        query_heads = rounded(jnp.dot(normed, enc_qkv[0], preferred_element_type=jnp.float32)).astype(jnp.float32).reshape(SEQ, HEADS, HEAD_DIM)
        key_heads = rounded(jnp.dot(normed, enc_qkv[1], preferred_element_type=jnp.float32)).astype(jnp.float32).reshape(SEQ, HEADS, HEAD_DIM)
        value_heads = rounded(jnp.dot(normed, enc_qkv[2], preferred_element_type=jnp.float32)).astype(jnp.float32).reshape(SEQ, HEADS, HEAD_DIM)
        scores = jnp.einsum('ihd,jhd->hij', query_heads, key_heads, precision=HIGHEST) + pair_bias
        valid_keys = positions < length
        scores = jnp.where(valid_keys[None, None, :], scores, MASKED)
        weights = jnp.exp(scores - lax.optimization_barrier(jnp.max(scores, axis=-1, keepdims=True)))
        probabilities = rounded(weights / lax.optimization_barrier(jnp.sum(weights, axis=-1, keepdims=True))).astype(jnp.float32)
        attended = rounded(jnp.einsum('hij,jhd->ihd', probabilities, value_heads, precision=HIGHEST)).astype(jnp.float32)
        attended = attended.reshape(SEQ, N_MP, group_cols)
        partials = rounded(jnp.einsum('sgc,gcd->gsd', attended, out_groups, precision=HIGHEST)).astype(jnp.float32)
        encoded = (passage.astype(jnp.float32) + lax.optimization_barrier(jnp.sum(partials, axis=0))).astype(jnp.bfloat16)
        memory = rms_norm(encoded, final_gain).astype(jnp.bfloat16)
        cross_keys = jnp.dot(memory, cross_keyval[0], preferred_element_type=jnp.float32).reshape(SEQ, HEADS, HEAD_DIM)
        cross_values = jnp.dot(memory, cross_keyval[1], preferred_element_type=jnp.float32).reshape(SEQ, HEADS, HEAD_DIM)
        cross_scores = jnp.einsum('rhd,jhd->rhj', cquery, cross_keys, precision=HIGHEST) + score_bias
        usable = ((positions[None, :] < length) & (row_claim[:, None] == owner_claim))[:, None, :]
        masked = jnp.where(usable, cross_scores, MASKED)
        new_max = jnp.maximum(run_max, lax.optimization_barrier(jnp.max(masked, axis=-1)))
        shrink = jnp.exp(run_max - new_max)
        weights_c = jnp.where(usable, jnp.exp(masked - new_max[..., None]), 0.0)
        run_total = run_total * shrink + lax.optimization_barrier(jnp.sum(weights_c, axis=-1))
        run_acc = run_acc * shrink[..., None] + jnp.einsum('rhj,jhd->rhd', weights_c, cross_values, precision=HIGHEST)
        return ((new_max, run_total, run_acc), encoded)
    start_state = (jnp.full((query_rows, HEADS), MASKED, jnp.float32), jnp.zeros((query_rows, HEADS), jnp.float32), jnp.zeros((query_rows, HEADS, HEAD_DIM), jnp.float32))
    final_state, encoded = lax.scan(passage_step, start_state, (tokens.reshape(PASSAGES, SEQ, D), lengths, assignment, retrieval))
    cross_attn = (final_state[2] / final_state[1][..., None]).reshape(query_rows, INNER)
    decoded = (embedded.astype(jnp.float32) + jnp.dot(cross_attn, cross_output.astype(jnp.float32), precision=HIGHEST)).astype(jnp.bfloat16)
    return (encoded.reshape(TOKENS, D), decoded.reshape(CLAIMS, POS, D))
```

```python
import functools
import math

import jax
import jax.numpy as jnp
import numpy as np
from jax import lax
from jax.experimental import pallas as pl
from jax.experimental.pallas import tpu as pltpu
from jax.sharding import PartitionSpec as P

D = 4096
HEAD_DIM = 64
BUCKETS = 32
MAXDIST = 128
SEQ = 256
CLAIMS = 4
POS = 2


EPSILON = 1e-06
MASKED = -1e30
HIGHEST = lax.Precision.HIGHEST
F32 = jnp.float32
BF16 = jnp.bfloat16
LANES = 128


def bucket_onehot(length, buckets, max_distance):
    halfway = buckets // 2
    exact_max = halfway // 2
    relative_list = list(range(-(length - 1), length))
    beyond_list = [
        min(
            halfway - 1,
            exact_max
            + math.floor(
                math.log(max(abs(shift), 1) / exact_max)
                / math.log(max_distance / exact_max)
                * (halfway - exact_max)
            ),
        )
        for shift in relative_list
    ]
    relative = np.array(relative_list)
    beyond = np.array(beyond_list)
    distance = np.abs(relative)
    bucket_ids = np.where(relative > 0, halfway, 0) + np.where(
        distance < exact_max, distance, beyond
    )
    return (bucket_ids[None, :] == np.arange(buckets)[:, None]).astype(np.float32)


def after(values, gate):
    return lax.optimization_barrier((values, gate))[0]


def split3(value):
    high = value.astype(BF16)
    rest = value - high.astype(F32)
    middle = rest.astype(BF16)
    low = (rest - middle.astype(F32)).astype(BF16)
    return high, middle, low


class Ring:
    def __init__(self, size):
        self.size = size
        order = list(range(0, size, 2)) + list(range(size - 1, 0, -2))
        self.forward = [(order[i], order[(i + 1) % size]) for i in range(size)]
        self.backward = [(b, a) for a, b in self.forward]
        table = np.zeros((size, size), np.int32)
        for place, device in enumerate(order):
            table[device] = [order[(place - step) % size] for step in range(size)]
        self.table = table

    def origins(self, index):
        return lax.dynamic_index_in_dim(jnp.asarray(self.table), index, 0, keepdims=False)


def norm_kernel(table_ref, tok_ref, gain_ref, out_ref):
    blocks = table_ref.shape[0]
    rows, model = tok_ref.shape
    width = model // blocks
    squares = jnp.zeros((rows, 1), F32)
    for block in range(blocks):
        wide = tok_ref[:, block * width : (block + 1) * width].astype(F32)
        squares = squares + jnp.sum(wide * wide, axis=1, keepdims=True)
    inverse = lax.rsqrt(squares / model + EPSILON)
    for block in range(blocks):
        at = pl.ds(pl.multiple_of(table_ref[block] * width, width), width)
        out_ref[:, block * width : (block + 1) * width] = (
            tok_ref[:, at].astype(F32) * inverse * gain_ref[:, at]
        ).astype(BF16)


def norm_in_order(table, tokens, gain):
    rows, model = tokens.shape
    spec = pl.BlockSpec((SEQ, model), lambda i, t: (i, 0))
    return pl.pallas_call(
        norm_kernel,
        out_shape=jax.ShapeDtypeStruct((rows, model), BF16),
        grid_spec=pltpu.PrefetchScalarGridSpec(
            num_scalar_prefetch=1,
            grid=(rows // SEQ,),
            in_specs=[spec, pl.BlockSpec((1, model), lambda i, t: (0, 0))],
            out_specs=spec,
        ),
        cost_estimate=pl.CostEstimate(
            flops=6 * rows * model, bytes_accessed=4 * rows * model, transcendentals=rows
        ),
    )(table, tokens, gain)


def bias_kernel(table_ref, out_ref):
    length = out_ref.shape[1]
    spread = jnp.broadcast_to(table_ref[0], (length, table_ref.shape[2]))
    rolled = pltpu.roll(spread, length + 1, 1, stride=1, stride_axis=0)
    out_ref[0] = rolled[:, :length]


def toeplitz(vectors):
    heads, width = vectors.shape
    length = width // 2
    return pl.pallas_call(
        bias_kernel,
        out_shape=jax.ShapeDtypeStruct((heads, length, length), F32),
        grid=(heads,),
        in_specs=[pl.BlockSpec((1, 1, width), lambda h: (h, 0, 0))],
        out_specs=pl.BlockSpec((1, length, length), lambda h: (h, 0, 0)),
    )(vectors.reshape(heads, 1, width))


TILE = 16


def lookup_kernel(ids_ref, limits_ref, table_ref, out_ref):
    row = pl.program_id(0)
    index = ids_ref[row] - limits_ref[0]
    inside = jnp.logical_and(index >= 0, index < limits_ref[1])
    offset = jnp.where(inside, lax.rem(jnp.maximum(index, 0), TILE), -1)
    found = table_ref[...].astype(F32)
    place = lax.broadcasted_iota(jnp.int32, found.shape, 0)
    found = jnp.sum(jnp.where(place == offset, found, 0.0), axis=0, keepdims=True)
    rows = lax.broadcasted_iota(jnp.int32, out_ref.shape, 0)
    kept = jnp.where(row == 0, jnp.zeros_like(found), 1.0)
    out_ref[...] = jnp.where(rows == row, found, jnp.where(kept > 0, out_ref[...], 0.0))


def lookup(ids, start, table):
    count = ids.shape[0]
    vocab, width = table.shape
    limits = jnp.stack([start, jnp.int32(vocab)])

    def block(r, ids_ref, limits_ref):
        index = jnp.clip(ids_ref[r] - limits_ref[0], 0, vocab - 1)
        return (index // TILE, 0)

    return pl.pallas_call(
        lookup_kernel,
        out_shape=jax.ShapeDtypeStruct((count, width), F32),
        grid_spec=pltpu.PrefetchScalarGridSpec(
            num_scalar_prefetch=2,
            grid=(count,),
            in_specs=[pl.BlockSpec((TILE, width), block)],
            out_specs=pl.BlockSpec((count, width), lambda r, i, l: (0, 0)),
        ),
    )(ids, limits, table)


def attend_kernel(lengths_ref, first_ref, second_ref, bias_ref, out_ref, *, start):
    rows = first_ref.shape[0]
    width = first_ref.shape[1] // 3
    length = lengths_ref[pl.program_id(0) + start]
    keys = lax.broadcasted_iota(jnp.int32, (rows, rows), 1)
    valid = keys < length
    low_half = lax.broadcasted_iota(jnp.int32, (rows, LANES), 1) < HEAD_DIM
    for half, source in enumerate((first_ref, second_ref)):
        for pair in range(width // LANES):
            query = source[:, pair * LANES : (pair + 1) * LANES].astype(F32)
            key = source[:, width + pair * LANES : width + (pair + 1) * LANES]
            value = source[:, 2 * width + pair * LANES : 2 * width + (pair + 1) * LANES]
            parts = []
            for side in range(2):
                head = half * (width // HEAD_DIM) + pair * 2 + side
                mine = low_half if side == 0 else jnp.logical_not(low_half)
                masked_query = jnp.where(mine, query, 0.0).astype(BF16)
                scores = lax.dot_general(
                    masked_query, key, (((1,), (1,)), ((), ())), preferred_element_type=F32
                )
                scores = jnp.where(valid, scores + bias_ref[head], MASKED)
                weights = jnp.exp(scores - jnp.max(scores, axis=1, keepdims=True))
                total = jnp.sum(weights, axis=1, keepdims=True)
                probabilities = (weights * (1.0 / total)).astype(BF16)
                parts.append(jnp.dot(probabilities, value, preferred_element_type=F32))
            column = half * width + pair * LANES
            out_ref[:, column : column + LANES] = jnp.where(low_half, parts[0], parts[1]).astype(
                BF16
            )


def attend(lengths, first, second, bias, start, count):
    width = first.shape[1] // 3
    spec = pl.BlockSpec((SEQ, first.shape[1]), lambda i, n: (i + start, 0))
    heads = bias.shape[0]
    return pl.pallas_call(
        functools.partial(attend_kernel, start=start),
        out_shape=jax.ShapeDtypeStruct((count * SEQ, 2 * width), BF16),
        grid_spec=pltpu.PrefetchScalarGridSpec(
            num_scalar_prefetch=1,
            grid=(count,),
            in_specs=[spec, spec, pl.BlockSpec((heads, SEQ, SEQ), lambda i, n: (0, 0, 0))],
            out_specs=pl.BlockSpec((SEQ, 2 * width), lambda i, n: (i, 0)),
        ),
        cost_estimate=pl.CostEstimate(
            flops=count * heads * SEQ * SEQ * 4 * LANES,
            bytes_accessed=count * SEQ * 16 * width + heads * SEQ * SEQ * 4,
            transcendentals=count * heads * SEQ * SEQ,
        ),
    )(lengths, first, second, bias)


def early_blocks(size):
    late = sorted({1, size - 1})
    return [j for j in range(size) if j not in late], late


def cross_kernel(
    table_ref, length_ref, bonus_ref, tok_ref, most_ref, rest_ref, gain_ref, folded_ref,
    enc_ref, out_ref, memory_ref,
):
    groups = most_ref.shape[0]
    blocks = out_ref.shape[0] // groups
    heads = out_ref.shape[1]
    width = folded_ref.shape[2]
    piece = width // groups
    rows = tok_ref.shape[0]
    squares = jnp.zeros((rows, 1), F32)
    for source, kept in zip((most_ref, rest_ref), early_blocks(blocks)):
        for place, block in enumerate(kept):
            at = pl.ds(pl.multiple_of(table_ref[block] * width, width), width)
            added = jnp.concatenate(
                [
                    source[group, :, place * piece : (place + 1) * piece].astype(F32)
                    for group in range(groups)
                ],
                axis=1,
            )
            encoded = (tok_ref[:, at].astype(F32) + added).astype(BF16)
            enc_ref[:, at] = encoded
            wide = encoded.astype(F32)
            squares = squares + jnp.sum(wide * wide, axis=1, keepdims=True)
    inverse = lax.rsqrt(squares / (blocks * width) + EPSILON)
    scores = [jnp.zeros((heads, rows), F32) for _ in range(groups)]
    for block in range(blocks):
        at = block * width
        memory = (
            enc_ref[:, at : at + width].astype(F32) * inverse * gain_ref[:, at : at + width]
        ).astype(BF16)
        memory_ref[:, at : at + width] = memory
        for group in range(groups):
            scores[group] = scores[group] + lax.dot_general(
                folded_ref[block * groups + group],
                memory,
                (((1,), (1,)), ((), ())),
                preferred_element_type=F32,
            )
    scores = jnp.concatenate(scores, axis=0)
    keys = lax.broadcasted_iota(jnp.int32, scores.shape, 1)
    usable = keys < length_ref[0]
    scores = jnp.where(usable, scores, MASKED)
    peak = jnp.max(scores, axis=1, keepdims=True)
    weights = jnp.where(usable, jnp.exp(scores - peak), 0.0)
    total = jnp.sum(weights, axis=1, keepdims=True)
    high = weights.astype(BF16)
    low = (weights - high.astype(F32)).astype(BF16)
    scale = 1.0 / total
    mass = peak + jnp.log(total) + bonus_ref[0]
    one, two, three = split3(mass)
    lane = lax.broadcasted_iota(jnp.int32, (groups * heads, LANES), 1)
    packed = jnp.where(
        lane == 0,
        one.astype(F32),
        jnp.where(lane == 1, two.astype(F32), jnp.where(lane == 2, three.astype(F32), 0.0)),
    ).astype(BF16)
    for block in range(blocks):
        memory = memory_ref[:, block * width : (block + 1) * width]
        pooled = jnp.dot(high, memory, preferred_element_type=F32) + jnp.dot(
            low, memory, preferred_element_type=F32
        )
        pooled = (pooled * scale).astype(BF16)
        for group in range(groups):
            out_ref[block * groups + group, :, :width] = pooled[
                group * heads : (group + 1) * heads
            ]
            out_ref[block * groups + group, :, width:] = packed[
                group * heads : (group + 1) * heads
            ]


def cross(table, length, bonus, tok, most, rest, gain, folded):
    rows, model = tok.shape
    devices, heads, width = folded.shape
    smem = pl.BlockSpec(memory_space=pltpu.SMEM)
    vmem = pl.BlockSpec(memory_space=pltpu.VMEM)
    return pl.pallas_call(
        cross_kernel,
        out_shape=(
            jax.ShapeDtypeStruct((rows, model), BF16),
            jax.ShapeDtypeStruct((devices, heads, width + LANES), BF16),
        ),
        in_specs=[smem, smem, smem, vmem, vmem, vmem, vmem, vmem],
        out_specs=(vmem, vmem),
        scratch_shapes=[pltpu.VMEM((rows, model), BF16)],
        cost_estimate=pl.CostEstimate(
            flops=6 * devices * heads * rows * width,
            bytes_accessed=rows * model * 6,
            transcendentals=devices * heads,
        ),
    )(table, length, bonus, tok, most, rest, gain, folded)


def split2(value):
    high = value.astype(BF16)
    return high, (value - high.astype(F32)).astype(BF16)


def combine_kernel(owner_ref, got_ref, weight_ref, out_ref):
    passages, rows, padded = got_ref.shape
    width = padded - LANES
    heads = rows // POS
    packed = got_ref[:, :, width:].reshape(passages * rows, LANES)
    pooled = got_ref[:, :, :width].reshape(passages * rows, width)
    picker = (lax.broadcasted_iota(jnp.int32, (8, LANES), 1) < 3).astype(BF16)
    mass = lax.dot_general(
        picker, packed, (((1,), (1,)), ((), ())), preferred_element_type=F32
    )[0:1]
    shape = (CLAIMS * rows, passages * rows)
    row = lax.broadcasted_iota(jnp.int32, shape, 0)
    column = lax.broadcasted_iota(jnp.int32, shape, 1)
    mine = jnp.logical_and(
        owner_ref[...] == row // rows, lax.rem(row, rows) == lax.rem(column, rows)
    )
    mass = jnp.where(mine, mass, MASKED)
    peak = jnp.max(mass, axis=1, keepdims=True)
    share = jnp.where(mine, jnp.exp(mass - peak), 0.0)
    total = jnp.sum(share, axis=1, keepdims=True)
    joint = jnp.zeros((CLAIMS * rows, width), F32)
    for part in split2(share):
        joint = joint + jnp.dot(part, pooled, preferred_element_type=F32)
    joint = joint / total
    weight = weight_ref[...]
    value = jnp.zeros((CLAIMS * rows, weight.shape[1]), F32)
    for part in split2(joint):
        value = value + jnp.dot(part, weight, preferred_element_type=F32)
    head = lax.broadcasted_iota(jnp.int32, value.shape, 1) // HEAD_DIM
    own = head == lax.rem(lax.broadcasted_iota(jnp.int32, value.shape, 0), heads)
    value = jnp.where(own, value, 0.0).reshape(CLAIMS * POS, heads, weight.shape[1])
    out_ref[...] = jnp.sum(value, axis=1)


def combine(owner, got, weight):
    vmem = pl.BlockSpec(memory_space=pltpu.VMEM)
    return pl.pallas_call(
        combine_kernel,
        out_shape=jax.ShapeDtypeStruct((CLAIMS * POS, weight.shape[1]), F32),
        in_specs=[vmem, vmem, vmem],
        out_specs=vmem,
    )(owner, got, weight)


def shards(
    tokens,
    lengths,
    assignment,
    retrieval,
    enc_gain,
    enc_qkv,
    position_bias,
    enc_output,
    final_gain,
    embedding,
    dec_tokens,
    dec_gain,
    cross_query,
    cross_keyval,
    cross_output,
):
    tok_rows, model_width = tokens.shape
    passages_here = lengths.shape[0]
    width_here = enc_qkv.shape[1]
    inner_here = enc_qkv.shape[2]
    heads_here = inner_here // HEAD_DIM
    query_rows = CLAIMS * POS
    psg = lax.axis_size("psg")
    groups = lax.axis_size("mp")
    assert passages_here == groups
    here = lax.axis_index("psg")
    group = lax.axis_index("mp")
    piece = width_here // groups
    ring = Ring(psg)
    table = ring.origins(here)

    def swap(value, k):
        return lax.ppermute(value, "mp", [(i, i ^ k) for i in range(groups)])

    half = inner_here // 2
    first_block = jnp.concatenate([enc_qkv[k][:, :half] for k in range(3)], axis=1)
    second_block = jnp.concatenate([enc_qkv[k][:, half:] for k in range(3)], axis=1)
    tokens_after = after(tokens, (first_block, second_block))
    normed = norm_in_order(table, tokens_after, enc_gain.reshape(1, -1))

    def term(block, place):
        part = normed[:, place * width_here : (place + 1) * width_here]
        return jnp.dot(part, block, preferred_element_type=F32)

    first_acc = term(first_block, 0)
    second_acc = term(second_block, 0)
    for step in range(1, psg):
        first_block = lax.ppermute(first_block, "psg", ring.forward)
        second_block = lax.ppermute(second_block, "psg", ring.backward)
        first_acc = lax.optimization_barrier(first_acc) + term(first_block, step)
        second_acc = lax.optimization_barrier(second_acc) + term(second_block, psg - step)
    first_heads = first_acc.astype(BF16)
    second_heads = second_acc.astype(BF16)

    found = lookup(dec_tokens.reshape(-1), group * embedding.shape[0], embedding).astype(BF16)
    found_all = lax.all_to_all(
        jnp.broadcast_to(found[None], (groups,) + found.shape), "mp", 0, 0, tiled=True
    )
    embedded = jnp.sum(found_all.astype(F32), axis=0)
    query_part = jnp.dot(
        embedded * dec_gain, cross_query.astype(F32), precision=HIGHEST
    )
    extra = jnp.concatenate(
        [jnp.sum(embedded * embedded, axis=1), assignment.astype(F32)]
    )
    extra = jnp.pad(extra, (0, inner_here - extra.shape[0]))
    message = jnp.concatenate(
        [query_part, jnp.broadcast_to(extra[None], (8, inner_here))], axis=0
    )
    messages = lax.all_to_all(
        jnp.broadcast_to(message[None], (psg,) + message.shape), "psg", 0, 0, tiled=True
    )
    joined = jnp.sum(messages[:, : query_rows + 1], axis=0)
    inverse_dec = lax.rsqrt(joined[query_rows, :query_rows] / D + EPSILON)
    cquery = (joined[:query_rows] * inverse_dec[:, None]).reshape(
        query_rows, heads_here, HEAD_DIM
    )
    owners = messages[:, query_rows, query_rows : query_rows + passages_here].reshape(-1)
    owners = (owners + 0.5).astype(jnp.int32)
    key_weight = cross_keyval[0].astype(F32).reshape(width_here, heads_here, HEAD_DIM)
    folded = jnp.einsum("rhj,dhj->rhd", cquery, key_weight, precision=HIGHEST).astype(BF16)
    chosen = (owners[:, None] == jnp.arange(CLAIMS)[None, :]).astype(BF16)
    to_send = jnp.dot(
        chosen, folded.reshape(CLAIMS, -1), preferred_element_type=F32
    ).astype(BF16)
    to_send = to_send.reshape(psg * groups, POS * heads_here, width_here)
    folded_here = lax.all_to_all(to_send, ("psg", "mp"), 0, 0, tiled=True)

    bias_table = jnp.dot(
        position_bias, jnp.asarray(np.pad(bucket_onehot(SEQ, BUCKETS, MAXDIST), ((0, 0), (0, 1)))),
        precision=HIGHEST,
    )
    pair_bias = toeplitz(bias_table)
    near, across = 1, groups // 2
    close, other = [], []
    per_call = passages_here // 2
    for start in range(0, passages_here, per_call):
        mine = attend(lengths, first_heads, second_heads, pair_bias, start, per_call)
        both = jnp.concatenate([mine, swap(mine, across)], axis=1)
        close.append(both)
        other.append(swap(both, near))
    close = jnp.concatenate(close, axis=0)
    other = jnp.concatenate(other, axis=0)

    turned = enc_output.T
    pieces = []
    for k in (0, across, near, across ^ near):
        block = lax.dynamic_slice_in_dim(turned, (group ^ k) * piece, piece, 0)
        pieces.append(block if k == 0 else swap(block, k))
    up = [jnp.concatenate(pieces[:2], axis=1)]
    down = [jnp.concatenate(pieces[2:], axis=1)]
    up[0], down[0] = after((up[0], down[0]), (first_block, second_block))
    for step in range(1, psg):
        up.append(lax.ppermute(up[-1], "psg", ring.forward))
        down.append(lax.ppermute(down[-1], "psg", ring.backward))
    contract = (((1,), (1,)), ((), ()))
    sums = []
    for blocks in early_blocks(psg):
        left = jnp.concatenate([up[j] for j in blocks], axis=0)
        right = jnp.concatenate([down[(psg - j) % psg] for j in blocks], axis=0)
        total = lax.dot_general(close, left, contract, preferred_element_type=F32)
        total = total + lax.dot_general(other, right, contract, preferred_element_type=F32)
        total = total.astype(BF16).reshape(groups, SEQ, len(blocks) * piece)
        sums.append(lax.all_to_all(total, "mp", 0, 0, tiled=True))

    own_tokens = lax.dynamic_slice_in_dim(tokens, group * SEQ, SEQ, 0)
    own_length = lax.dynamic_slice_in_dim(lengths, group, 1, 0)
    own_bonus = lax.dynamic_slice_in_dim(retrieval, group, 1, 0)
    rows, pooled = cross(
        table, own_length, own_bonus, own_tokens, *sums, final_gain.reshape(1, -1), folded_here
    )
    got = lax.all_to_all(pooled, ("psg", "mp"), 0, 0, tiled=True)
    share = model_width // groups
    encoded = lax.all_to_all(
        rows.reshape(SEQ, groups, share).transpose(1, 0, 2), "mp", 0, 0, tiled=True
    ).reshape(tok_rows, share)
    owner_row = jnp.repeat(owners, POS * heads_here).reshape(1, -1)
    value_part = combine(owner_row, got, cross_keyval[1])
    values = lax.all_to_all(
        jnp.broadcast_to(value_part[None], (psg,) + value_part.shape), "psg", 0, 0, tiled=True
    )
    cross_attn = jnp.sum(values, axis=0)
    out_part = jnp.dot(cross_attn, cross_output.astype(F32), precision=HIGHEST)
    out_part, encoded = lax.optimization_barrier((out_part, encoded))
    out_parts = lax.all_to_all(
        out_part.reshape(query_rows, groups, piece).transpose(1, 0, 2), "mp", 0, 0, tiled=True
    )
    residual = lax.dynamic_slice_in_dim(embedded, group * piece, piece, 1)
    decoded = (residual + jnp.sum(out_parts, axis=0)).astype(BF16).reshape(CLAIMS, POS, piece)
    return (encoded, decoded)


def solution(mesh):
    in_specs = (
        P("psg", None),
        P("psg"),
        P("psg"),
        P("psg"),
        P(),
        P(None, "psg", "mp"),
        P("mp", None),
        P("mp", "psg"),
        P(),
        P("mp", "psg"),
        P(),
        P("psg"),
        P("psg", "mp"),
        P(None, "psg", "mp"),
        P("mp", "psg"),
    )
    out_specs = (P("psg", "mp"), P(None, None, ("psg", "mp")))
    return jax.shard_map(shards, mesh=mesh, in_specs=in_specs, out_specs=out_specs, check_vma=False)
```

```python
import functools
import math

import jax
import jax.numpy as jnp
import numpy as np
from jax import lax
from jax.experimental import pallas as pl
from jax.experimental.pallas import tpu as pltpu
from jax.sharding import PartitionSpec as P


D = 4096
HEAD_DIM = 64
BUCKETS = 32
MAXDIST = 128
SEQ = 256
CLAIMS = 4
POS = 2


EPSILON = 1e-06
MASKED = -1e30
HIGHEST = lax.Precision.HIGHEST
F32 = jnp.float32
BF16 = jnp.bfloat16
LANES = 128


def bucket_onehot(length, buckets, max_distance):
    halfway = buckets // 2
    exact_max = halfway // 2
    relative_list = list(range(-(length - 1), length))
    beyond_list = [
        min(
            halfway - 1,
            exact_max
            + math.floor(
                math.log(max(abs(shift), 1) / exact_max)
                / math.log(max_distance / exact_max)
                * (halfway - exact_max)
            ),
        )
        for shift in relative_list
    ]
    relative = np.array(relative_list)
    beyond = np.array(beyond_list)
    distance = np.abs(relative)
    bucket_ids = np.where(relative > 0, halfway, 0) + np.where(
        distance < exact_max, distance, beyond
    )
    return (bucket_ids[None, :] == np.arange(buckets)[:, None]).astype(np.float32)


def after(values, gate):
    return lax.optimization_barrier((values, gate))[0]


def split3(value):
    high = value.astype(BF16)
    rest = value - high.astype(F32)
    middle = rest.astype(BF16)
    low = (rest - middle.astype(F32)).astype(BF16)
    return high, middle, low


class Ring:
    def __init__(self, size):
        self.size = size
        order = list(range(0, size, 2)) + list(range(size - 1, 0, -2))
        self.forward = [(order[i], order[(i + 1) % size]) for i in range(size)]
        self.backward = [(b, a) for a, b in self.forward]
        table = np.zeros((size, size), np.int32)
        for place, device in enumerate(order):
            table[device] = [order[(place - step) % size] for step in range(size)]
        self.tables = np.concatenate([table, np.argsort(table, axis=1).astype(np.int32)], axis=1)

    def origins(self, index):
        both = lax.dynamic_index_in_dim(jnp.asarray(self.tables), index, 0, keepdims=False)
        return both[: self.size], both[self.size :]


def norm_kernel(table_ref, tok_ref, gain_ref, out_ref):
    blocks = table_ref.shape[0]
    rows, model = tok_ref.shape
    width = model // blocks
    squares = jnp.zeros((rows, 1), F32)
    for block in range(blocks):
        wide = tok_ref[:, block * width : (block + 1) * width].astype(F32)
        squares = squares + jnp.sum(wide * wide, axis=1, keepdims=True)
    inverse = lax.rsqrt(squares / model + EPSILON)
    for block in range(blocks):
        at = pl.ds(pl.multiple_of(table_ref[block] * width, width), width)
        out_ref[:, block * width : (block + 1) * width] = (
            tok_ref[:, at].astype(F32) * inverse * gain_ref[:, at]
        ).astype(BF16)


def norm_in_order(table, tokens, gain):
    rows, model = tokens.shape
    spec = pl.BlockSpec((SEQ, model), lambda i, t: (i, 0))
    return pl.pallas_call(
        norm_kernel,
        out_shape=jax.ShapeDtypeStruct((rows, model), BF16),
        grid_spec=pltpu.PrefetchScalarGridSpec(
            num_scalar_prefetch=1,
            grid=(rows // SEQ,),
            in_specs=[spec, pl.BlockSpec((1, model), lambda i, t: (0, 0))],
            out_specs=spec,
        ),
        cost_estimate=pl.CostEstimate(
            flops=6 * rows * model, bytes_accessed=4 * rows * model, transcendentals=rows
        ),
    )(table, tokens, gain)


def bias_kernel(table_ref, out_ref):
    length = out_ref.shape[1]
    spread = jnp.broadcast_to(table_ref[0], (length, table_ref.shape[2]))
    rolled = pltpu.roll(spread, length + 1, 1, stride=1, stride_axis=0)
    out_ref[0] = rolled[:, :length]


def toeplitz(vectors):
    heads, width = vectors.shape
    length = width // 2
    return pl.pallas_call(
        bias_kernel,
        out_shape=jax.ShapeDtypeStruct((heads, length, length), F32),
        grid=(heads,),
        in_specs=[pl.BlockSpec((1, 1, width), lambda h: (h, 0, 0))],
        out_specs=pl.BlockSpec((1, length, length), lambda h: (h, 0, 0)),
    )(vectors.reshape(heads, 1, width))


TILE = 16


def lookup_kernel(ids_ref, limits_ref, table_ref, out_ref):
    row = pl.program_id(0)
    index = ids_ref[row] - limits_ref[0]
    inside = jnp.logical_and(index >= 0, index < limits_ref[1])
    offset = jnp.where(inside, lax.rem(jnp.maximum(index, 0), TILE), -1)
    found = table_ref[...].astype(F32)
    place = lax.broadcasted_iota(jnp.int32, found.shape, 0)
    found = jnp.sum(jnp.where(place == offset, found, 0.0), axis=0, keepdims=True)
    rows = lax.broadcasted_iota(jnp.int32, out_ref.shape, 0)
    kept = jnp.where(row == 0, jnp.zeros_like(found), 1.0)
    out_ref[...] = jnp.where(rows == row, found, jnp.where(kept > 0, out_ref[...], 0.0))


def lookup(ids, start, table):
    count = ids.shape[0]
    vocab, width = table.shape
    limits = jnp.stack([start, jnp.int32(vocab)])

    def block(r, ids_ref, limits_ref):
        index = jnp.clip(ids_ref[r] - limits_ref[0], 0, vocab - 1)
        return (index // TILE, 0)

    return pl.pallas_call(
        lookup_kernel,
        out_shape=jax.ShapeDtypeStruct((count, width), F32),
        grid_spec=pltpu.PrefetchScalarGridSpec(
            num_scalar_prefetch=2,
            grid=(count,),
            in_specs=[pl.BlockSpec((TILE, width), block)],
            out_specs=pl.BlockSpec((count, width), lambda r, i, l: (0, 0)),
        ),
    )(ids, limits, table)


def attend_kernel(lengths_ref, group_ref, bias_ref, *refs, away):
    count = len(away)
    for at, k in enumerate(away):
        length = lengths_ref[group_ref[0] ^ k]
        attend_passage(length, refs[2 * at], refs[2 * at + 1], bias_ref, refs[2 * count + at])


def attend_passage(length, first_ref, second_ref, bias_ref, out_ref):
    rows = first_ref.shape[0]
    width = first_ref.shape[1] // 3
    keys = lax.broadcasted_iota(jnp.int32, (rows, rows), 1)
    valid = keys < length
    low_half = lax.broadcasted_iota(jnp.int32, (rows, LANES), 1) < HEAD_DIM
    for half, source in enumerate((first_ref, second_ref)):
        for pair in range(width // LANES):
            query = source[:, pair * LANES : (pair + 1) * LANES].astype(F32)
            key = source[:, width + pair * LANES : width + (pair + 1) * LANES]
            value = source[:, 2 * width + pair * LANES : 2 * width + (pair + 1) * LANES]
            parts = []
            for side in range(2):
                head = half * (width // HEAD_DIM) + pair * 2 + side
                mine = low_half if side == 0 else jnp.logical_not(low_half)
                masked_query = jnp.where(mine, query, 0.0).astype(BF16)
                scores = lax.dot_general(
                    masked_query, key, (((1,), (1,)), ((), ())), preferred_element_type=F32
                )
                scores = jnp.where(valid, scores + bias_ref[head], MASKED)
                weights = jnp.exp(scores - jnp.max(scores, axis=1, keepdims=True))
                total = jnp.sum(weights, axis=1, keepdims=True)
                probabilities = (weights * (1.0 / total)).astype(BF16)
                parts.append(jnp.dot(probabilities, value, preferred_element_type=F32))
            column = half * width + pair * LANES
            out_ref[:, column : column + LANES] = jnp.where(low_half, parts[0], parts[1]).astype(
                BF16
            )


def attend(lengths, group, first, second, bias, away):
    width = first.shape[1] // 3
    heads = bias.shape[0]
    count = len(away)
    specs = []
    for k in away:
        specs += [pl.BlockSpec((SEQ, first.shape[1]), lambda i, n, g, k=k: (g[0] ^ k, 0))] * 2
    return pl.pallas_call(
        functools.partial(attend_kernel, away=tuple(away)),
        out_shape=[jax.ShapeDtypeStruct((SEQ, 2 * width), BF16)] * count,
        grid_spec=pltpu.PrefetchScalarGridSpec(
            num_scalar_prefetch=2,
            grid=(1,),
            in_specs=[pl.BlockSpec((heads, SEQ, SEQ), lambda i, n, g: (0, 0, 0))] + specs,
            out_specs=[pl.BlockSpec((SEQ, 2 * width), lambda i, n, g: (0, 0))] * count,
        ),
        cost_estimate=pl.CostEstimate(
            flops=count * heads * SEQ * SEQ * 4 * LANES,
            bytes_accessed=count * SEQ * 16 * width + heads * SEQ * SEQ * 4,
            transcendentals=count * heads * SEQ * SEQ,
        ),
    )(lengths, group, bias, *([first, second] * count))


def join_kernel(*refs):
    out_ref = refs[-1]
    count = (len(refs) - 1) // 2
    cut, width = refs[0].shape
    for j in range(count):
        out_ref[:cut, j * width : (j + 1) * width] = refs[j][...]
        out_ref[cut:, j * width : (j + 1) * width] = refs[count + j][...]


def join(uppers, lowers):
    cut, width = uppers[0].shape
    vmem = pl.BlockSpec(memory_space=pltpu.VMEM)
    shape = (2 * cut, width * len(uppers))
    return pl.pallas_call(
        join_kernel,
        out_shape=jax.ShapeDtypeStruct(shape, uppers[0].dtype),
        in_specs=[vmem] * (2 * len(uppers)),
        out_specs=vmem,
        cost_estimate=pl.CostEstimate(
            flops=0, bytes_accessed=4 * shape[0] * shape[1], transcendentals=0
        ),
    )(*uppers, *lowers)


def project_kernel(step_ref, group_ref, tok_ref, *refs):
    groups = (len(refs)) // 3
    total = jnp.zeros(tok_ref.shape, F32)
    for term, weight in zip(refs[:groups], refs[groups : 2 * groups]):
        partial = jnp.dot(term[...], weight[...], preferred_element_type=F32)
        total = total + partial.astype(BF16).astype(F32)
    encoded = (tok_ref[...].astype(F32) + total).astype(BF16)
    for k, out_ref in enumerate(refs[2 * groups :]):

        @pl.when(pl.program_id(0) == k)
        def _(out_ref=out_ref):
            out_ref[...] = encoded


def project(step_of, group, tokens, terms, weights, width):
    groups = len(terms)
    model = tokens.shape[1]
    share = model // groups
    rows, depth = terms[0].shape
    blocks = share // width

    def column(i, j, g):
        return (i ^ g[0]) * blocks + j

    def place(k):
        return lambda i, j, t, g: (
            0,
            jnp.where(i < k, 0, jnp.where(i > k, blocks - 1, j)),
        )

    return pl.pallas_call(
        project_kernel,
        out_shape=[jax.ShapeDtypeStruct((rows, share), BF16)] * groups,
        grid_spec=pltpu.PrefetchScalarGridSpec(
            num_scalar_prefetch=2,
            grid=(groups, blocks),
            in_specs=[pl.BlockSpec((rows, width), lambda i, j, t, g: (g[0], column(i, j, g)))]
            + [pl.BlockSpec((rows, depth), lambda i, j, t, g: (0, 0))] * groups
            + [pl.BlockSpec((depth, width), lambda i, j, t, g: (0, t[column(i, j, g)]))] * groups,
            out_specs=[pl.BlockSpec((rows, width), place(k)) for k in range(groups)],
        ),
        cost_estimate=pl.CostEstimate(
            flops=2 * rows * groups * depth * model,
            bytes_accessed=2 * groups * depth * model + 4 * rows * model,
            transcendentals=0,
        ),
    )(step_of, group, tokens, *terms, *weights)


def cross_kernel(
    group_ref, length_ref, bonus_ref, gain_ref, folded_ref, *refs
):
    enc_refs, out_ref, memory_ref = refs[:-2], refs[-2], refs[-1]
    groups = len(enc_refs)
    rows, share = enc_refs[0].shape
    blocks = out_ref.shape[0] // groups
    heads = out_ref.shape[1]
    width = folded_ref.shape[2]
    per = share // width
    passage = group_ref[0]
    squares = jnp.zeros((rows, 1), F32)
    for enc_ref in enc_refs:
        for part in range(per):
            wide = enc_ref[:, part * width : (part + 1) * width].astype(F32)
            squares = squares + jnp.sum(wide * wide, axis=1, keepdims=True)
    inverse = lax.rsqrt(squares / (blocks * width) + EPSILON)
    scores = [jnp.zeros((heads, rows), F32) for _ in range(groups)]
    for k, enc_ref in enumerate(enc_refs):
        for part in range(per):
            block = (passage ^ k) * per + part
            gain = gain_ref[:, pl.ds(pl.multiple_of(block * width, width), width)]
            wide = enc_ref[:, part * width : (part + 1) * width].astype(F32)
            memory = (wide * inverse * gain).astype(BF16)
            at = (k * per + part) * width
            memory_ref[:, at : at + width] = memory
            for group in range(groups):
                scores[group] = scores[group] + lax.dot_general(
                    folded_ref[block * groups + group],
                    memory,
                    (((1,), (1,)), ((), ())),
                    preferred_element_type=F32,
                )
    scores = jnp.concatenate(scores, axis=0)
    keys = lax.broadcasted_iota(jnp.int32, scores.shape, 1)
    usable = keys < length_ref[passage]
    scores = jnp.where(usable, scores, MASKED)
    peak = jnp.max(scores, axis=1, keepdims=True)
    weights = jnp.where(usable, jnp.exp(scores - peak), 0.0)
    total = jnp.sum(weights, axis=1, keepdims=True)
    high = weights.astype(BF16)
    low = (weights - high.astype(F32)).astype(BF16)
    scale = 1.0 / total
    mass = peak + jnp.log(total) + bonus_ref[passage]
    one, two, three = split3(mass)
    lane = lax.broadcasted_iota(jnp.int32, (groups * heads, LANES), 1)
    packed = jnp.where(
        lane == 0,
        one.astype(F32),
        jnp.where(lane == 1, two.astype(F32), jnp.where(lane == 2, three.astype(F32), 0.0)),
    ).astype(BF16)
    for place in range(blocks):
        block = (passage ^ (place // per)) * per + place % per
        memory = memory_ref[:, place * width : (place + 1) * width]
        pooled = jnp.dot(high, memory, preferred_element_type=F32) + jnp.dot(
            low, memory, preferred_element_type=F32
        )
        pooled = (pooled * scale).astype(BF16)
        for group in range(groups):
            out_ref[block * groups + group, :, :width] = pooled[
                group * heads : (group + 1) * heads
            ]
            out_ref[block * groups + group, :, width:] = packed[
                group * heads : (group + 1) * heads
            ]


def cross(group, lengths, bonus, encoded, gain, folded):
    groups = len(encoded)
    rows, share = encoded[0].shape
    model = groups * share
    devices, heads, width = folded.shape
    smem = pl.BlockSpec(memory_space=pltpu.SMEM)
    vmem = pl.BlockSpec(memory_space=pltpu.VMEM)
    return pl.pallas_call(
        cross_kernel,
        out_shape=jax.ShapeDtypeStruct((devices, heads, width + LANES), BF16),
        in_specs=[smem, smem, smem] + [vmem] * (2 + groups),
        out_specs=vmem,
        scratch_shapes=[pltpu.VMEM((rows, model), BF16)],
        cost_estimate=pl.CostEstimate(
            flops=6 * devices * heads * rows * width,
            bytes_accessed=rows * model * 2,
            transcendentals=devices * heads,
        ),
    )(group, lengths, bonus, gain, folded, *encoded)


def gather_kernel(group_ref, *refs):
    out_ref = refs[-1]
    for k, ref in enumerate(refs[:-1]):

        @pl.when(pl.program_id(0) == k)
        def _(ref=ref):
            out_ref[...] = ref[...]


def in_passage_order(group, blocks):
    rows, width = blocks[0].shape
    return pl.pallas_call(
        gather_kernel,
        out_shape=jax.ShapeDtypeStruct((len(blocks) * rows, width), blocks[0].dtype),
        grid_spec=pltpu.PrefetchScalarGridSpec(
            num_scalar_prefetch=1,
            grid=(len(blocks),),
            in_specs=[pl.BlockSpec((rows, width), lambda i, g: (0, 0))] * len(blocks),
            out_specs=pl.BlockSpec((rows, width), lambda i, g: (g[0] ^ i, 0)),
        ),
    )(group, *blocks)


def split2(value):
    high = value.astype(BF16)
    return high, (value - high.astype(F32)).astype(BF16)


def combine_kernel(owner_ref, got_ref, weight_ref, out_ref):
    passages, rows, padded = got_ref.shape
    width = padded - LANES
    heads = rows // POS
    packed = got_ref[:, :, width:].reshape(passages * rows, LANES)
    pooled = got_ref[:, :, :width].reshape(passages * rows, width)
    picker = (lax.broadcasted_iota(jnp.int32, (8, LANES), 1) < 3).astype(BF16)
    mass = lax.dot_general(
        picker, packed, (((1,), (1,)), ((), ())), preferred_element_type=F32
    )[0:1]
    shape = (CLAIMS * rows, passages * rows)
    row = lax.broadcasted_iota(jnp.int32, shape, 0)
    column = lax.broadcasted_iota(jnp.int32, shape, 1)
    mine = jnp.logical_and(
        owner_ref[...] == row // rows, lax.rem(row, rows) == lax.rem(column, rows)
    )
    mass = jnp.where(mine, mass, MASKED)
    peak = jnp.max(mass, axis=1, keepdims=True)
    share = jnp.where(mine, jnp.exp(mass - peak), 0.0)
    total = jnp.sum(share, axis=1, keepdims=True)
    joint = jnp.zeros((CLAIMS * rows, width), F32)
    for part in split2(share):
        joint = joint + jnp.dot(part, pooled, preferred_element_type=F32)
    joint = joint / total
    weight = weight_ref[...]
    value = jnp.zeros((CLAIMS * rows, weight.shape[1]), F32)
    for part in split2(joint):
        value = value + jnp.dot(part, weight, preferred_element_type=F32)
    head = lax.broadcasted_iota(jnp.int32, value.shape, 1) // HEAD_DIM
    own = head == lax.rem(lax.broadcasted_iota(jnp.int32, value.shape, 0), heads)
    value = jnp.where(own, value, 0.0).reshape(CLAIMS * POS, heads, weight.shape[1])
    value = jnp.sum(value, axis=1)
    for copy in range(out_ref.shape[0]):
        out_ref[copy] = value


def combine(owner, got, weight, copies):
    vmem = pl.BlockSpec(memory_space=pltpu.VMEM)
    return pl.pallas_call(
        combine_kernel,
        out_shape=jax.ShapeDtypeStruct((copies, CLAIMS * POS, weight.shape[1]), F32),
        in_specs=[vmem, vmem, vmem],
        out_specs=vmem,
    )(owner, got, weight)


def program(
    tokens,
    lengths,
    assignment,
    retrieval,
    enc_gain,
    enc_qkv,
    position_bias,
    enc_output,
    final_gain,
    embedding,
    dec_tokens,
    dec_gain,
    cross_query,
    cross_keyval,
    cross_output,
):
    passages_here = lengths.shape[0]
    width_here = enc_qkv.shape[1]
    inner_here = enc_qkv.shape[2]
    heads_here = inner_here // HEAD_DIM
    query_rows = CLAIMS * POS
    psg = lax.axis_size("psg")
    groups = lax.axis_size("mp")
    assert passages_here == groups
    here = lax.axis_index("psg")
    group = lax.axis_index("mp")
    piece = width_here // groups
    ring = Ring(psg)
    table, step_of = ring.origins(here)

    def swap(value, k):
        return lax.ppermute(value, "mp", [(i, i ^ k) for i in range(groups)])

    here_1 = group.reshape(1)
    across, near = groups // 2, 1
    order = [across, across ^ near, near, 0]

    cut = enc_output.shape[0] // 2
    up, down = [enc_output[:cut]], [enc_output[cut:]]
    for _ in range(1, psg):
        up.append(lax.ppermute(up[-1], "psg", ring.forward))
        down.append(lax.ppermute(down[-1], "psg", ring.backward))
    own_rows = join(up, [down[(psg - j) % psg] for j in range(psg)])
    far_rows = swap(own_rows, across)
    near_rows = swap(own_rows, near)
    corner_rows = swap(far_rows, near)
    out_weights = [far_rows, corner_rows, near_rows, own_rows]

    half = inner_here // 2
    first_block = jnp.concatenate([enc_qkv[k][:, :half] for k in range(3)], axis=1)
    second_block = jnp.concatenate([enc_qkv[k][:, half:] for k in range(3)], axis=1)
    first_block, second_block = after(
        (first_block, second_block), (up[psg - 2], down[psg - 2])
    )
    normed = norm_in_order(table, tokens, enc_gain.reshape(1, -1))

    def term(block, place):
        part = normed[:, place * width_here : (place + 1) * width_here]
        return jnp.dot(part, block, preferred_element_type=F32)

    own_blocks = (first_block, second_block)
    arrived = [own_blocks]
    late = (psg - 1) // 2
    for step in range(1, psg):
        first_block = lax.ppermute(first_block, "psg", ring.forward)
        second_block = lax.ppermute(second_block, "psg", ring.backward)
        arrived.append((first_block, second_block))
        first_term = term(first_block, step)
        second_term = term(second_block, psg - step)
        if step > 1:
            first_term = lax.optimization_barrier(first_acc) + first_term
            second_term = lax.optimization_barrier(second_acc) + second_term
        first_acc, second_acc = first_term, second_term
        if step == late:
            first_acc = lax.optimization_barrier(first_acc) + term(own_blocks[0], 0)
            second_acc = lax.optimization_barrier(second_acc) + term(own_blocks[1], 0)
        if step == psg - 1:
            first_acc = first_acc.astype(BF16)
            second_acc = second_acc.astype(BF16)
    first_heads, second_heads = first_acc, second_acc

    found = lookup(dec_tokens.reshape(-1), group * embedding.shape[0], embedding)
    found = found.astype(BF16)
    found_all = lax.all_to_all(
        jnp.broadcast_to(found[None], (groups,) + found.shape), "mp", 0, 0, tiled=True
    )
    embedded = jnp.sum(found_all.astype(F32), axis=0)
    query_part = jnp.dot(
        embedded * dec_gain, cross_query.astype(F32), precision=HIGHEST
    )
    extra = jnp.concatenate(
        [jnp.sum(embedded * embedded, axis=1), assignment.astype(F32)]
    )
    extra = jnp.pad(extra, (0, inner_here - extra.shape[0]))
    message = jnp.concatenate(
        [query_part, jnp.broadcast_to(extra[None], (8, inner_here))], axis=0
    )
    messages = lax.all_to_all(
        jnp.broadcast_to(message[None], (psg,) + message.shape), "psg", 0, 0, tiled=True
    )
    messages = after(messages, arrived[min(4, psg - 1)])
    joined = jnp.sum(messages[:, : query_rows + 1], axis=0)
    inverse_dec = lax.rsqrt(joined[query_rows, :query_rows] / D + EPSILON)
    cquery = (joined[:query_rows] * inverse_dec[:, None]).reshape(
        query_rows, heads_here, HEAD_DIM
    )
    owners = messages[:, query_rows, query_rows : query_rows + passages_here].reshape(-1)
    owners = (owners + 0.5).astype(jnp.int32)
    key_weight = cross_keyval[0].astype(F32).reshape(width_here, heads_here, HEAD_DIM)
    folded = jnp.einsum("rhj,dhj->rhd", cquery, key_weight, precision=HIGHEST).astype(BF16)
    chosen = (owners[:, None] == jnp.arange(CLAIMS)[None, :]).astype(BF16)
    to_send = jnp.dot(
        chosen, folded.reshape(CLAIMS, -1), preferred_element_type=F32
    ).astype(BF16)
    to_send = to_send.reshape(psg * groups, POS * heads_here, width_here)
    folded_here = lax.all_to_all(to_send, ("psg", "mp"), 0, 0, tiled=True)

    bias_table = jnp.dot(
        position_bias, jnp.asarray(np.pad(bucket_onehot(SEQ, BUCKETS, MAXDIST), ((0, 0), (0, 1)))),
        precision=HIGHEST,
    )
    pair_bias = toeplitz(bias_table)
    terms = []
    for call in range(0, groups, 2):
        ks = order[call : call + 2]
        outs = attend(lengths, here_1, first_heads, second_heads, pair_bias, ks)
        terms += [swap(out, k) if k else out for out, k in zip(outs, ks)]
    rows = project(step_of, here_1, tokens, terms, out_weights, width_here)

    pooled = cross(
        here_1, lengths, retrieval, rows, final_gain.reshape(1, -1), folded_here
    )
    got = lax.all_to_all(pooled, ("psg", "mp"), 0, 0, tiled=True)
    blocks = [swap(rows[k], k) if k else rows[0] for k in range(groups)]
    encoded = in_passage_order(here_1, blocks)
    owner_row = jnp.repeat(owners, POS * heads_here).reshape(1, -1)
    value_part = combine(owner_row, got, cross_keyval[1], psg)
    values = lax.all_to_all(value_part, "psg", 0, 0, tiled=True)
    cross_attn = jnp.sum(values, axis=0)
    out_part = jnp.dot(cross_attn, cross_output.astype(F32), precision=HIGHEST)
    out_parts = lax.all_to_all(
        out_part.reshape(query_rows, groups, piece).transpose(1, 0, 2), "mp", 0, 0, tiled=True
    )
    residual = lax.dynamic_slice_in_dim(embedded, group * piece, piece, 1)
    decoded = (residual + jnp.sum(out_parts, axis=0)).astype(BF16).reshape(CLAIMS, POS, piece)
    return (encoded, decoded)


def solution(mesh):
    in_specs = (
        P("psg", None),
        P("psg"),
        P("psg"),
        P("psg"),
        P(),
        P(None, "psg", "mp"),
        P("mp", None),
        P("mp", "psg"),
        P(),
        P("mp", "psg"),
        P(),
        P("psg"),
        P("psg", "mp"),
        P(None, "psg", "mp"),
        P("mp", "psg"),
    )
    out_specs = (P("psg", "mp"), P(None, None, ("psg", "mp")))
    return jax.shard_map(program, mesh=mesh, in_specs=in_specs, out_specs=out_specs, check_vma=False)
```

```python
import functools
import math

import jax
import jax.numpy as jnp
import numpy as np
from jax import lax
from jax.experimental import pallas as pl
from jax.experimental.pallas import tpu as pltpu
from jax.sharding import PartitionSpec as P


D = 4096
HEAD_DIM = 64
BUCKETS = 32
MAXDIST = 128
SEQ = 256
CLAIMS = 4
POS = 2


EPSILON = 1e-06
MASKED = -1e30
HIGHEST = lax.Precision.HIGHEST
F32 = jnp.float32
BF16 = jnp.bfloat16
LANES = 128
MIB = 1 << 20


def bucket_onehot(length, buckets, max_distance):
    halfway = buckets // 2
    exact_max = halfway // 2
    relative_list = list(range(-(length - 1), length))
    beyond_list = [
        min(
            halfway - 1,
            exact_max
            + math.floor(
                math.log(max(abs(shift), 1) / exact_max)
                / math.log(max_distance / exact_max)
                * (halfway - exact_max)
            ),
        )
        for shift in relative_list
    ]
    relative = np.array(relative_list)
    beyond = np.array(beyond_list)
    distance = np.abs(relative)
    bucket_ids = np.where(relative > 0, halfway, 0) + np.where(
        distance < exact_max, distance, beyond
    )
    return (bucket_ids[None, :] == np.arange(buckets)[:, None]).astype(np.float32)


def after(values, gate):
    return lax.optimization_barrier((values, gate))[0]


def split3(value):
    high = value.astype(BF16)
    rest = value - high.astype(F32)
    middle = rest.astype(BF16)
    low = (rest - middle.astype(F32)).astype(BF16)
    return high, middle, low


class Ring:
    def __init__(self, size):
        self.size = size
        order = list(range(0, size, 2)) + list(range(size - 1, 0, -2))
        self.forward = [(order[i], order[(i + 1) % size]) for i in range(size)]
        self.backward = [(b, a) for a, b in self.forward]
        table = np.zeros((size, size), np.int32)
        for place, device in enumerate(order):
            table[device] = [order[(place - step) % size] for step in range(size)]
        self.tables = np.concatenate([table, np.argsort(table, axis=1).astype(np.int32)], axis=1)

    def origins(self, index):
        both = lax.dynamic_index_in_dim(jnp.asarray(self.tables), index, 0, keepdims=False)
        return both[: self.size], both[self.size :]


def norm_kernel(table_ref, tok_ref, gain_ref, out_ref):
    blocks = table_ref.shape[0]
    rows, model = tok_ref.shape
    width = model // blocks
    squares = jnp.zeros((rows, 1), F32)
    for block in range(blocks):
        wide = tok_ref[:, block * width : (block + 1) * width].astype(F32)
        squares = squares + jnp.sum(wide * wide, axis=1, keepdims=True)
    inverse = lax.rsqrt(squares / model + EPSILON)
    for block in range(blocks):
        at = pl.ds(pl.multiple_of(table_ref[block] * width, width), width)
        out_ref[:, block * width : (block + 1) * width] = (
            tok_ref[:, at].astype(F32) * inverse * gain_ref[:, at]
        ).astype(BF16)


def norm_in_order(table, tokens, gain):
    rows, model = tokens.shape
    spec = pl.BlockSpec((SEQ, model), lambda i, t: (i, 0))
    return pl.pallas_call(
        norm_kernel,
        compiler_params=pltpu.CompilerParams(vmem_limit_bytes=24 * MIB),
        out_shape=jax.ShapeDtypeStruct((rows, model), BF16),
        grid_spec=pltpu.PrefetchScalarGridSpec(
            num_scalar_prefetch=1,
            grid=(rows // SEQ,),
            in_specs=[spec, pl.BlockSpec((1, model), lambda i, t: (0, 0))],
            out_specs=spec,
        ),
        cost_estimate=pl.CostEstimate(
            flops=6 * rows * model, bytes_accessed=4 * rows * model, transcendentals=rows
        ),
    )(table, tokens, gain)


def bias_kernel(table_ref, out_ref):
    length = out_ref.shape[1]
    spread = jnp.broadcast_to(table_ref[0], (length, table_ref.shape[2]))
    rolled = pltpu.roll(spread, length + 1, 1, stride=1, stride_axis=0)
    out_ref[0] = rolled[:, :length]


def toeplitz(vectors):
    heads, width = vectors.shape
    length = width // 2
    return pl.pallas_call(
        bias_kernel,
        compiler_params=pltpu.CompilerParams(vmem_limit_bytes=8 * MIB),
        out_shape=jax.ShapeDtypeStruct((heads, length, length), F32),
        grid=(heads,),
        in_specs=[pl.BlockSpec((1, 1, width), lambda h: (h, 0, 0))],
        out_specs=pl.BlockSpec((1, length, length), lambda h: (h, 0, 0)),
    )(vectors.reshape(heads, 1, width))


TILE = 16


def lookup_kernel(ids_ref, limits_ref, table_ref, out_ref):
    row = pl.program_id(0)
    index = ids_ref[row] - limits_ref[0]
    inside = jnp.logical_and(index >= 0, index < limits_ref[1])
    offset = jnp.where(inside, lax.rem(jnp.maximum(index, 0), TILE), -1)
    found = table_ref[...].astype(F32)
    place = lax.broadcasted_iota(jnp.int32, found.shape, 0)
    found = jnp.sum(jnp.where(place == offset, found, 0.0), axis=0, keepdims=True)
    rows = lax.broadcasted_iota(jnp.int32, out_ref.shape, 0)
    kept = jnp.where(row == 0, jnp.zeros_like(found), 1.0)
    out_ref[...] = jnp.where(rows == row, found, jnp.where(kept > 0, out_ref[...], 0.0))


def lookup(ids, start, table):
    count = ids.shape[0]
    vocab, width = table.shape
    limits = jnp.stack([start, jnp.int32(vocab)])

    def block(r, ids_ref, limits_ref):
        index = jnp.clip(ids_ref[r] - limits_ref[0], 0, vocab - 1)
        return (index // TILE, 0)

    return pl.pallas_call(
        lookup_kernel,
        compiler_params=pltpu.CompilerParams(vmem_limit_bytes=8 * MIB),
        out_shape=jax.ShapeDtypeStruct((count, width), F32),
        grid_spec=pltpu.PrefetchScalarGridSpec(
            num_scalar_prefetch=2,
            grid=(count,),
            in_specs=[pl.BlockSpec((TILE, width), block)],
            out_specs=pl.BlockSpec((count, width), lambda r, i, l: (0, 0)),
        ),
    )(ids, limits, table)


def attend_kernel(lengths_ref, group_ref, bias_ref, *refs, away):
    count = len(away)
    for at, k in enumerate(away):
        length = lengths_ref[group_ref[0] ^ k]
        attend_passage(length, refs[2 * at], refs[2 * at + 1], bias_ref, refs[2 * count + at])


def attend_passage(length, first_ref, second_ref, bias_ref, out_ref):
    rows = first_ref.shape[0]
    width = first_ref.shape[1] // 3
    keys = lax.broadcasted_iota(jnp.int32, (rows, rows), 1)
    valid = keys < length
    low_half = lax.broadcasted_iota(jnp.int32, (rows, LANES), 1) < HEAD_DIM
    for half, source in enumerate((first_ref, second_ref)):
        for pair in range(width // LANES):
            query = source[:, pair * LANES : (pair + 1) * LANES].astype(F32)
            key = source[:, width + pair * LANES : width + (pair + 1) * LANES]
            value = source[:, 2 * width + pair * LANES : 2 * width + (pair + 1) * LANES]
            parts = []
            for side in range(2):
                head = half * (width // HEAD_DIM) + pair * 2 + side
                mine = low_half if side == 0 else jnp.logical_not(low_half)
                masked_query = jnp.where(mine, query, 0.0).astype(BF16)
                scores = lax.dot_general(
                    masked_query, key, (((1,), (1,)), ((), ())), preferred_element_type=F32
                )
                scores = jnp.where(valid, scores + bias_ref[head], MASKED)
                weights = jnp.exp(scores - jnp.max(scores, axis=1, keepdims=True))
                total = jnp.sum(weights, axis=1, keepdims=True)
                probabilities = (weights * (1.0 / total)).astype(BF16)
                parts.append(jnp.dot(probabilities, value, preferred_element_type=F32))
            column = half * width + pair * LANES
            out_ref[:, column : column + LANES] = jnp.where(low_half, parts[0], parts[1]).astype(
                BF16
            )


def attend(lengths, group, first, second, bias, away):
    width = first.shape[1] // 3
    heads = bias.shape[0]
    count = len(away)
    specs = []
    for k in away:
        specs += [pl.BlockSpec((SEQ, first.shape[1]), lambda i, n, g, k=k: (g[0] ^ k, 0))] * 2
    return pl.pallas_call(
        functools.partial(attend_kernel, away=tuple(away)),
        compiler_params=pltpu.CompilerParams(vmem_limit_bytes=24 * MIB),
        out_shape=[jax.ShapeDtypeStruct((SEQ, 2 * width), BF16)] * count,
        grid_spec=pltpu.PrefetchScalarGridSpec(
            num_scalar_prefetch=2,
            grid=(1,),
            in_specs=[pl.BlockSpec((heads, SEQ, SEQ), lambda i, n, g: (0, 0, 0))] + specs,
            out_specs=[pl.BlockSpec((SEQ, 2 * width), lambda i, n, g: (0, 0))] * count,
        ),
        cost_estimate=pl.CostEstimate(
            flops=count * heads * SEQ * SEQ * 4 * LANES,
            bytes_accessed=count * SEQ * 16 * width + heads * SEQ * SEQ * 4,
            transcendentals=count * heads * SEQ * SEQ,
        ),
    )(lengths, group, bias, *([first, second] * count))


def join_kernel(*refs):
    out_ref = refs[-1]
    count = (len(refs) - 1) // 2
    cut, width = refs[0].shape
    for j in range(count):
        out_ref[:cut, j * width : (j + 1) * width] = refs[j][...]
        out_ref[cut:, j * width : (j + 1) * width] = refs[count + j][...]


def join(uppers, lowers):
    cut, width = uppers[0].shape
    vmem = pl.BlockSpec(memory_space=pltpu.VMEM)
    shape = (2 * cut, width * len(uppers))
    return pl.pallas_call(
        join_kernel,
        compiler_params=pltpu.CompilerParams(vmem_limit_bytes=16 * MIB),
        out_shape=jax.ShapeDtypeStruct(shape, uppers[0].dtype),
        in_specs=[vmem] * (2 * len(uppers)),
        out_specs=vmem,
        cost_estimate=pl.CostEstimate(
            flops=0, bytes_accessed=4 * shape[0] * shape[1], transcendentals=0
        ),
    )(*uppers, *lowers)


def project_kernel(step_ref, group_ref, tok_ref, *refs):
    groups = (len(refs)) // 3
    total = jnp.zeros(tok_ref.shape, F32)
    for term, weight in zip(refs[:groups], refs[groups : 2 * groups]):
        partial = jnp.dot(term[...], weight[...], preferred_element_type=F32)
        total = total + partial.astype(BF16).astype(F32)
    encoded = (tok_ref[...].astype(F32) + total).astype(BF16)
    for k, out_ref in enumerate(refs[2 * groups :]):

        @pl.when(pl.program_id(0) == k)
        def _(out_ref=out_ref):
            out_ref[...] = encoded


def project(step_of, group, tokens, terms, weights, width):
    groups = len(terms)
    model = tokens.shape[1]
    share = model // groups
    rows, depth = terms[0].shape
    blocks = share // width

    def column(i, j, g):
        return (i ^ g[0]) * blocks + j

    def place(k):
        return lambda i, j, t, g: (
            0,
            jnp.where(i < k, 0, jnp.where(i > k, blocks - 1, j)),
        )

    return pl.pallas_call(
        project_kernel,
        compiler_params=pltpu.CompilerParams(vmem_limit_bytes=58 * MIB),
        out_shape=[jax.ShapeDtypeStruct((rows, share), BF16)] * groups,
        grid_spec=pltpu.PrefetchScalarGridSpec(
            num_scalar_prefetch=2,
            grid=(groups, blocks),
            in_specs=[pl.BlockSpec((rows, width), lambda i, j, t, g: (g[0], column(i, j, g)))]
            + [pl.BlockSpec((rows, depth), lambda i, j, t, g: (0, 0))] * groups
            + [pl.BlockSpec((depth, width), lambda i, j, t, g: (0, t[column(i, j, g)]))] * groups,
            out_specs=[pl.BlockSpec((rows, width), place(k)) for k in range(groups)],
        ),
        cost_estimate=pl.CostEstimate(
            flops=2 * rows * groups * depth * model,
            bytes_accessed=2 * groups * depth * model + 4 * rows * model,
            transcendentals=0,
        ),
    )(step_of, group, tokens, *terms, *weights)


def cross_kernel(
    group_ref, length_ref, bonus_ref, gain_ref, folded_ref, *refs
):
    enc_refs, out_ref, memory_ref = refs[:-2], refs[-2], refs[-1]
    groups = len(enc_refs)
    rows, share = enc_refs[0].shape
    blocks = out_ref.shape[0] // groups
    heads = out_ref.shape[1]
    width = folded_ref.shape[2]
    per = share // width
    passage = group_ref[0]
    squares = jnp.zeros((rows, 1), F32)
    for enc_ref in enc_refs:
        for part in range(per):
            wide = enc_ref[:, part * width : (part + 1) * width].astype(F32)
            squares = squares + jnp.sum(wide * wide, axis=1, keepdims=True)
    inverse = lax.rsqrt(squares / (blocks * width) + EPSILON)
    scores = [jnp.zeros((heads, rows), F32) for _ in range(groups)]
    for k, enc_ref in enumerate(enc_refs):
        for part in range(per):
            block = (passage ^ k) * per + part
            gain = gain_ref[:, pl.ds(pl.multiple_of(block * width, width), width)]
            wide = enc_ref[:, part * width : (part + 1) * width].astype(F32)
            memory = (wide * inverse * gain).astype(BF16)
            at = (k * per + part) * width
            memory_ref[:, at : at + width] = memory
            for group in range(groups):
                scores[group] = scores[group] + lax.dot_general(
                    folded_ref[block * groups + group],
                    memory,
                    (((1,), (1,)), ((), ())),
                    preferred_element_type=F32,
                )
    scores = jnp.concatenate(scores, axis=0)
    keys = lax.broadcasted_iota(jnp.int32, scores.shape, 1)
    usable = keys < length_ref[passage]
    scores = jnp.where(usable, scores, MASKED)
    peak = jnp.max(scores, axis=1, keepdims=True)
    weights = jnp.where(usable, jnp.exp(scores - peak), 0.0)
    total = jnp.sum(weights, axis=1, keepdims=True)
    high = weights.astype(BF16)
    low = (weights - high.astype(F32)).astype(BF16)
    scale = 1.0 / total
    mass = peak + jnp.log(total) + bonus_ref[passage]
    one, two, three = split3(mass)
    lane = lax.broadcasted_iota(jnp.int32, (groups * heads, LANES), 1)
    packed = jnp.where(
        lane == 0,
        one.astype(F32),
        jnp.where(lane == 1, two.astype(F32), jnp.where(lane == 2, three.astype(F32), 0.0)),
    ).astype(BF16)
    for place in range(blocks):
        block = (passage ^ (place // per)) * per + place % per
        memory = memory_ref[:, place * width : (place + 1) * width]
        pooled = jnp.dot(high, memory, preferred_element_type=F32) + jnp.dot(
            low, memory, preferred_element_type=F32
        )
        pooled = (pooled * scale).astype(BF16)
        for group in range(groups):
            out_ref[block * groups + group, :, :width] = pooled[
                group * heads : (group + 1) * heads
            ]
            out_ref[block * groups + group, :, width:] = packed[
                group * heads : (group + 1) * heads
            ]


def cross(group, lengths, bonus, encoded, gain, folded):
    groups = len(encoded)
    rows, share = encoded[0].shape
    model = groups * share
    devices, heads, width = folded.shape
    smem = pl.BlockSpec(memory_space=pltpu.SMEM)
    vmem = pl.BlockSpec(memory_space=pltpu.VMEM)
    return pl.pallas_call(
        cross_kernel,
        compiler_params=pltpu.CompilerParams(vmem_limit_bytes=24 * MIB),
        out_shape=jax.ShapeDtypeStruct((devices, heads, width + LANES), BF16),
        in_specs=[smem, smem, smem] + [vmem] * (2 + groups),
        out_specs=vmem,
        scratch_shapes=[pltpu.VMEM((rows, model), BF16)],
        cost_estimate=pl.CostEstimate(
            flops=6 * devices * heads * rows * width,
            bytes_accessed=rows * model * 2,
            transcendentals=devices * heads,
        ),
    )(group, lengths, bonus, gain, folded, *encoded)


def gather_kernel(group_ref, *refs):
    out_ref = refs[-1]
    for k, ref in enumerate(refs[:-1]):

        @pl.when(pl.program_id(0) == k)
        def _(ref=ref):
            out_ref[...] = ref[...]


def in_passage_order(group, blocks):
    rows, width = blocks[0].shape
    return pl.pallas_call(
        gather_kernel,
        compiler_params=pltpu.CompilerParams(vmem_limit_bytes=8 * MIB),
        out_shape=jax.ShapeDtypeStruct((len(blocks) * rows, width), blocks[0].dtype),
        grid_spec=pltpu.PrefetchScalarGridSpec(
            num_scalar_prefetch=1,
            grid=(len(blocks),),
            in_specs=[pl.BlockSpec((rows, width), lambda i, g: (0, 0))] * len(blocks),
            out_specs=pl.BlockSpec((rows, width), lambda i, g: (g[0] ^ i, 0)),
        ),
    )(group, *blocks)


def split2(value):
    high = value.astype(BF16)
    return high, (value - high.astype(F32)).astype(BF16)


def combine_kernel(owner_ref, got_ref, weight_ref, out_ref):
    passages, rows, padded = got_ref.shape
    width = padded - LANES
    heads = rows // POS
    packed = got_ref[:, :, width:].reshape(passages * rows, LANES)
    pooled = got_ref[:, :, :width].reshape(passages * rows, width)
    picker = (lax.broadcasted_iota(jnp.int32, (8, LANES), 1) < 3).astype(BF16)
    mass = lax.dot_general(
        picker, packed, (((1,), (1,)), ((), ())), preferred_element_type=F32
    )[0:1]
    shape = (CLAIMS * rows, passages * rows)
    row = lax.broadcasted_iota(jnp.int32, shape, 0)
    column = lax.broadcasted_iota(jnp.int32, shape, 1)
    mine = jnp.logical_and(
        owner_ref[...] == row // rows, lax.rem(row, rows) == lax.rem(column, rows)
    )
    mass = jnp.where(mine, mass, MASKED)
    peak = jnp.max(mass, axis=1, keepdims=True)
    share = jnp.where(mine, jnp.exp(mass - peak), 0.0)
    total = jnp.sum(share, axis=1, keepdims=True)
    joint = jnp.zeros((CLAIMS * rows, width), F32)
    for part in split2(share):
        joint = joint + jnp.dot(part, pooled, preferred_element_type=F32)
    joint = joint / total
    weight = weight_ref[...]
    value = jnp.zeros((CLAIMS * rows, weight.shape[1]), F32)
    for part in split2(joint):
        value = value + jnp.dot(part, weight, preferred_element_type=F32)
    head = lax.broadcasted_iota(jnp.int32, value.shape, 1) // HEAD_DIM
    own = head == lax.rem(lax.broadcasted_iota(jnp.int32, value.shape, 0), heads)
    value = jnp.where(own, value, 0.0).reshape(CLAIMS * POS, heads, weight.shape[1])
    value = jnp.sum(value, axis=1).astype(BF16)
    for copy in range(out_ref.shape[0]):
        out_ref[copy] = value


def combine(owner, got, weight, copies):
    vmem = pl.BlockSpec(memory_space=pltpu.VMEM)
    return pl.pallas_call(
        combine_kernel,
        compiler_params=pltpu.CompilerParams(vmem_limit_bytes=16 * MIB),
        out_shape=jax.ShapeDtypeStruct((copies, CLAIMS * POS, weight.shape[1]), BF16),
        in_specs=[vmem, vmem, vmem],
        out_specs=vmem,
    )(owner, got, weight)


def finish_kernel(group_ref, got_ref, residual_ref, *refs):
    weight_refs, out_ref = refs[:-1], refs[-1]
    groups = len(weight_refs)
    total = residual_ref[...]
    for k, weight_ref in enumerate(weight_refs):
        source = group_ref[0] ^ k
        value = jnp.zeros(got_ref.shape[1:], F32)
        for block in range(got_ref.shape[0] // groups):
            value = value + got_ref[block * groups + source].astype(F32)
        for part in split2(value):
            total = total + jnp.dot(part, weight_ref[...], preferred_element_type=F32)
    out_ref[...] = total.astype(BF16)


def finish(group, got, residual, weights):
    smem = pl.BlockSpec(memory_space=pltpu.SMEM)
    vmem = pl.BlockSpec(memory_space=pltpu.VMEM)
    return pl.pallas_call(
        finish_kernel,
        compiler_params=pltpu.CompilerParams(vmem_limit_bytes=8 * MIB),
        out_shape=jax.ShapeDtypeStruct(residual.shape, BF16),
        in_specs=[smem] + [vmem] * (2 + len(weights)),
        out_specs=vmem,
    )(group, got, residual, *weights)


def program(
    tokens,
    lengths,
    assignment,
    retrieval,
    enc_gain,
    enc_qkv,
    position_bias,
    enc_output,
    final_gain,
    embedding,
    dec_tokens,
    dec_gain,
    cross_query,
    cross_keyval,
    cross_output,
):
    passages_here = lengths.shape[0]
    width_here = enc_qkv.shape[1]
    inner_here = enc_qkv.shape[2]
    heads_here = inner_here // HEAD_DIM
    query_rows = CLAIMS * POS
    psg = lax.axis_size("psg")
    groups = lax.axis_size("mp")
    assert passages_here == groups
    here = lax.axis_index("psg")
    group = lax.axis_index("mp")
    piece = width_here // groups
    ring = Ring(psg)
    table, step_of = ring.origins(here)

    def swap(value, k):
        return lax.ppermute(value, "mp", [(i, i ^ k) for i in range(groups)])

    here_1 = group.reshape(1)
    across, near = groups // 2, 1
    order = [across, across ^ near, near, 0]

    cut = enc_output.shape[0] // 2
    up, down = [enc_output[:cut]], [enc_output[cut:]]
    for _ in range(1, psg):
        up.append(lax.ppermute(up[-1], "psg", ring.forward))
        down.append(lax.ppermute(down[-1], "psg", ring.backward))
    own_rows = join(up, [down[(psg - j) % psg] for j in range(psg)])
    far_rows = swap(own_rows, across)
    near_rows = swap(own_rows, near)
    corner_rows = swap(far_rows, near)
    out_weights = [far_rows, corner_rows, near_rows, own_rows]

    half = inner_here // 2
    first_block = jnp.concatenate([enc_qkv[k][:, :half] for k in range(3)], axis=1)
    second_block = jnp.concatenate([enc_qkv[k][:, half:] for k in range(3)], axis=1)
    first_block, second_block = after(
        (first_block, second_block), (up[psg - 2], down[psg - 2])
    )
    normed = norm_in_order(table, tokens, enc_gain.reshape(1, -1))

    def term(block, place):
        part = normed[:, place * width_here : (place + 1) * width_here]
        return jnp.dot(part, block, preferred_element_type=F32)

    own_blocks = (first_block, second_block)
    arrived = [own_blocks]
    late = psg - 3
    for step in range(1, psg):
        first_block = lax.ppermute(first_block, "psg", ring.forward)
        second_block = lax.ppermute(second_block, "psg", ring.backward)
        arrived.append((first_block, second_block))
        first_term = term(first_block, step)
        second_term = term(second_block, psg - step)
        if step > 1:
            first_term = lax.optimization_barrier(first_acc) + first_term
            second_term = lax.optimization_barrier(second_acc) + second_term
        first_acc, second_acc = first_term, second_term
        if step == late:
            first_acc = lax.optimization_barrier(first_acc) + term(own_blocks[0], 0)
            second_acc = lax.optimization_barrier(second_acc) + term(own_blocks[1], 0)
        if step == psg - 1:
            first_acc = first_acc.astype(BF16)
            second_acc = second_acc.astype(BF16)
    first_heads, second_heads = first_acc, second_acc

    found = lookup(dec_tokens.reshape(-1), group * embedding.shape[0], embedding)
    found = found.astype(BF16)
    found_all = lax.all_to_all(
        jnp.broadcast_to(found[None], (groups,) + found.shape), "mp", 0, 0, tiled=True
    )
    embedded = jnp.sum(found_all.astype(F32), axis=0)
    residual = lax.dynamic_slice_in_dim(embedded, group * piece, piece, 1)
    final_weights = []
    for k in range(groups):
        block = lax.dynamic_slice_in_dim(cross_output, (group ^ k) * piece, piece, 1)
        final_weights.append(swap(block, k) if k else block)
    query_part = jnp.dot(
        embedded * dec_gain, cross_query.astype(F32), precision=HIGHEST
    )
    extra = jnp.concatenate(
        [jnp.sum(embedded * embedded, axis=1), assignment.astype(F32)]
    )
    extra = jnp.pad(extra, (0, inner_here - extra.shape[0]))
    message = jnp.concatenate(
        [query_part, jnp.broadcast_to(extra[None], (8, inner_here))], axis=0
    )
    messages = lax.all_to_all(
        jnp.broadcast_to(message[None], (psg,) + message.shape), "psg", 0, 0, tiled=True
    )
    messages = after(messages, arrived[min(5, psg - 1)])
    joined = jnp.sum(messages[:, : query_rows + 1], axis=0)
    inverse_dec = lax.rsqrt(joined[query_rows, :query_rows] / D + EPSILON)
    cquery = (joined[:query_rows] * inverse_dec[:, None]).reshape(
        query_rows, heads_here, HEAD_DIM
    )
    owners = messages[:, query_rows, query_rows : query_rows + passages_here].reshape(-1)
    owners = (owners + 0.5).astype(jnp.int32)
    key_weight = cross_keyval[0].astype(F32).reshape(width_here, heads_here, HEAD_DIM)
    folded = jnp.einsum("rhj,dhj->rhd", cquery, key_weight, precision=HIGHEST).astype(BF16)
    chosen = (owners[:, None] == jnp.arange(CLAIMS)[None, :]).astype(BF16)
    to_send = jnp.dot(
        chosen, folded.reshape(CLAIMS, -1), preferred_element_type=F32
    ).astype(BF16)
    to_send = to_send.reshape(psg * groups, POS * heads_here, width_here)
    folded_here = lax.all_to_all(to_send, ("psg", "mp"), 0, 0, tiled=True)

    bias_table = jnp.dot(
        position_bias, jnp.asarray(np.pad(bucket_onehot(SEQ, BUCKETS, MAXDIST), ((0, 0), (0, 1)))),
        precision=HIGHEST,
    )
    pair_bias = toeplitz(bias_table)
    terms = []
    for call in range(0, groups, 2):
        ks = order[call : call + 2]
        outs = attend(lengths, here_1, first_heads, second_heads, pair_bias, ks)
        terms += [swap(out, k) if k else out for out, k in zip(outs, ks)]
    rows = project(step_of, here_1, tokens, terms, out_weights, width_here)

    pooled = cross(
        here_1, lengths, retrieval, rows, final_gain.reshape(1, -1), folded_here
    )
    got = lax.all_to_all(pooled, ("psg", "mp"), 0, 0, tiled=True)
    blocks = [swap(rows[k], k) if k else rows[0] for k in range(groups)]
    encoded = in_passage_order(here_1, blocks)
    owner_row = jnp.repeat(owners, POS * heads_here).reshape(1, -1)
    value_part = combine(owner_row, got, cross_keyval[1], psg * groups)
    values = lax.all_to_all(value_part, ("psg", "mp"), 0, 0, tiled=True)
    decoded = finish(here_1, values, residual, final_weights).reshape(CLAIMS, POS, piece)
    return (encoded, decoded)


def solution(mesh):
    in_specs = (
        P("psg", None),
        P("psg"),
        P("psg"),
        P("psg"),
        P(),
        P(None, "psg", "mp"),
        P("mp", None),
        P("mp", "psg"),
        P(),
        P("mp", "psg"),
        P(),
        P("psg"),
        P("psg", "mp"),
        P(None, "psg", "mp"),
        P("mp", "psg"),
    )
    out_specs = (P("psg", "mp"), P(None, None, ("psg", "mp")))
    return jax.shard_map(program, mesh=mesh, in_specs=in_specs, out_specs=out_specs, check_vma=False)
```
